512 devices in a mesh: mode: 64 (over y, z), rank: 8 (over x, core).
Axes of the slice: x: 4, y: 4, z: 16, core: 2. Of those that a mesh axis runs over, the one named last changes fastest.
Arguments:
- operator_cores: bfloat16 [2, 4, 4, 2048, 2048], P(None, None, None, 'mode'), may hold values from -0.26516504 to 0.26516504
- vector_cores: bfloat16 [2, 64, 64, 2048], P(None, 'rank', None, 'mode'), may hold values from -17 to 17
- left_gram: float32 [256, 256], replicated, may hold values from -330 to 330, as said below
- bases: float32 [3, 256, 64], replicated, may hold values from -0.375 to 0.375
Outputs:
- rounded_cores: float32 [2, 64, 2048, 64], P(None, None, ('mode', 'rank'))
- final_gram: float32 [256, 256], replicated
The draws below stay inside these ranges and needn't reach their ends.
Inputs may be any that keep to these rules, and one draw needn't show every extreme that they name: left_gram is symmetric positive definite.
All inputs are finite; a program needn't handle non-finite values.
Results may differ from the reference program's by a relative error of at most 0.0028.
Values may be sent and summed in bfloat16 or wider, within the bound.
A program may use at most 64 MiB of HBM per device.

```python
import jax
import jax.numpy as jnp
from jax import lax

MODES = 2048
OP_RANK = 4
VEC_RANK = 64
OUT_RANK = 64
CORES = 2
RANK = 256


def draw_operator_cores(key, part):
    first, second, third = jax.random.split(key, 3)
    shape = (CORES, OP_RANK, OP_RANK, MODES, MODES)
    shared_shape = (CORES, 1, 1, MODES, MODES)
    position = jnp.arange(MODES, dtype=jnp.float32) / (MODES - 1)
    base = jax.random.normal(first, shape, jnp.float32)
    shared = jax.random.normal(third, shared_shape, jnp.float32)
    ramp = 1.0 + 2.0 * position
    combined = jnp.clip((base + 0.5 * shared) / jnp.sqrt(jnp.float32(1.25)), -6.0, 6.0)
    rough = jnp.exp(jax.random.uniform(second, (CORES, 1, 1, MODES, 1), jnp.float32, -0.5, 0.5))
    scale = 1.0 / (2.5 * jnp.sqrt(jnp.float32(MODES)))
    return (combined * ramp[:, None] * rough * scale).astype(jnp.bfloat16)


def draw_vector_cores(key, part):
    first, second, third = jax.random.split(key, 3)
    shape = (CORES, VEC_RANK, VEC_RANK, MODES)
    base = jnp.clip(jax.random.normal(first, shape, jnp.float32), -6.0, 6.0)
    row_scale = jnp.exp(jax.random.uniform(second, (CORES, VEC_RANK, 1, 1), jnp.float32, -0.69, 0.69))
    mode_scale = jnp.exp(jax.random.uniform(third, (CORES, 1, 1, MODES), jnp.float32, -0.35, 0.35))
    return (base * row_scale * mode_scale).astype(jnp.bfloat16)


def draw_left_gram(key, part):
    first, second = jax.random.split(key, 2)
    factor = jax.random.normal(first, (RANK, 2 * RANK), jnp.float32)
    factor = jnp.clip(factor, -6.0, 6.0)
    product = jnp.dot(factor, factor.T, precision=lax.Precision.HIGHEST) / (2.0 * RANK)
    product = 0.5 * (product + product.T) + 0.5 * jnp.eye(RANK, dtype=jnp.float32)
    scales = jnp.exp(jax.random.uniform(second, (RANK,), jnp.float32, 0.0, 1.0986))
    return scales[:, None] * product * scales[None, :]


def centred(stream_key, extent, spread, bound, kind=jnp.bfloat16):
    return jnp.clip(spread * jax.random.normal(stream_key, extent, jnp.float32), -bound, bound).astype(kind)


def setup_inputs(seed: int = 0) -> dict:
    seeds = jax.random.split(jax.random.key(seed), 5)
    operator_cores = draw_operator_cores(jax.random.fold_in(seeds[4], 71), 0)
    vector_cores = draw_vector_cores(jax.random.fold_in(seeds[4], 71), 0)
    left_gram = draw_left_gram(jax.random.fold_in(seeds[4], 71), 0)
    bases = centred(seeds[3], (CORES + 1, RANK, OUT_RANK), RANK ** -0.5, 0.375, jnp.float32)
    return dict(operator_cores=operator_cores, vector_cores=vector_cores, left_gram=left_gram, bases=bases)


HIGHEST_PRECISION = lax.Precision.HIGHEST

def solve_mixing(gram_now, basis):
    projected = jnp.dot(basis.T.astype(jnp.float32), gram_now.astype(jnp.float32), precision=HIGHEST_PRECISION, preferred_element_type=jnp.float32)
    reduced = jnp.dot(projected.astype(jnp.float32), basis.astype(jnp.float32), precision=HIGHEST_PRECISION, preferred_element_type=jnp.float32)
    reduced = 0.5 * (reduced + reduced.T)
    lower_factor = jnp.linalg.cholesky(reduced)
    return jax.scipy.linalg.cho_solve((lower_factor, True), projected)

def reference(operator_cores, vector_cores, left_gram, bases):
    gram_now = left_gram
    results = []
    blocks = max(1, MODES // 128)
    width_block = MODES // blocks
    for core_index in range(CORES):
        mixing = solve_mixing(gram_now, bases[core_index])
        next_basis = bases[core_index + 1]
        vector_wide = vector_cores[core_index].astype(jnp.float32)
        operator_split = operator_cores[core_index].reshape(OP_RANK, OP_RANK, blocks, width_block, MODES)
        operator_split = operator_split.transpose(2, 0, 1, 3, 4)

        def mode_block(operator_block, gram_now=gram_now, mixing=mixing, next_basis=next_basis, vector_wide=vector_wide):
            product = jnp.einsum('qsj,ptij->qpist', vector_wide, operator_block.astype(jnp.float32))
            product = product.reshape(RANK, width_block, RANK)
            rounded = lax.optimization_barrier(product.astype(jnp.bfloat16))
            widened = rounded.astype(jnp.float32)
            weighted = jnp.einsum('ad,dib->aib', gram_now, widened, precision=HIGHEST_PRECISION)
            partial_gram = jnp.einsum('aib,aic->bc', widened, weighted, precision=HIGHEST_PRECISION)
            mixed = jnp.einsum('sa,aib->sib', mixing, widened, precision=HIGHEST_PRECISION)
            rounded_core = jnp.einsum('sib,bt->sit', mixed, next_basis, precision=HIGHEST_PRECISION)
            return (partial_gram, rounded_core)
        partials, pieces = lax.map(mode_block, operator_split)
        gram_now = jnp.sum(partials, axis=0) / (MODES * RANK)
        results.append(pieces.transpose(1, 0, 2, 3).reshape(OUT_RANK, MODES, OUT_RANK))
    return (jnp.stack(results), gram_now)
```

```python
import functools

import jax
import jax.numpy as jnp
from jax import lax
from jax.experimental import pallas as pl
from jax.experimental.pallas import tpu as pltpu
from jax.sharding import PartitionSpec as P

GRID_Y = 4
HIGHEST_PRECISION = lax.Precision.HIGHEST
MESH = pl.DeviceIdType.MESH
F32 = jnp.float32
BF16 = jnp.bfloat16


def solve_mixing(gram_now, basis):
    projected = jnp.dot(
        basis.T, gram_now, precision=HIGHEST_PRECISION, preferred_element_type=jnp.float32
    )
    reduced = jnp.dot(
        projected, basis, precision=HIGHEST_PRECISION, preferred_element_type=jnp.float32
    )
    reduced = 0.5 * (reduced + reduced.T)
    lower_factor = jnp.linalg.cholesky(reduced)
    return jax.scipy.linalg.cho_solve((lower_factor, True), projected)


def mm(a, b):
    return jnp.dot(a, b, preferred_element_type=F32)


def mm_nt(a, b):
    return lax.dot_general(a, b, (((1,), (1,)), ((), ())), preferred_element_type=F32)


def split(a):
    high = a.astype(BF16)
    return high, (a - high.astype(F32)).astype(BF16)


def one_hot(shape, target):
    rows = lax.broadcasted_iota(jnp.int32, shape, 0)
    columns = lax.broadcasted_iota(jnp.int32, shape, 1)
    return jnp.where(target(rows) == columns, 1.0, 0.0).astype(BF16)


def window_kernel(dims, *refs):
    (ny, nz, nr, lm, ql, vw, ow, rank) = dims
    (v_ref, o_hbm, g_ref, b_ref, q_out, gram_out,
     o_buf, vg, acc, s_buf, x_buf, y_buf, p_buf, pt_buf, part, ra, sb, rb, gram,
     o_sem, ys0, yr0, zs0, zr0, zs1, zr1, ys1, yr1, as_sem, ar_sem,
     a_s, a_r, b_s, b_r, c_s, c_r) = refs
    modes = ny * nz * lm
    ni = lm // nr
    rows = ow * ow * lm
    chunk = ow * ni
    no = ny * nr
    rb_rows = rank // no
    kr = nz // 2
    kl = nz - 1 - kr
    mode = lax.axis_index("mode")
    r = lax.axis_index("rank")
    y = mode // nz
    z = mode % nz
    o = y * nr + r
    right, left = (z + 1) % nz, (z + nz - 1) % nz

    def group(k):
        other = (o + k) % no
        return other, ((other // nr) * nz + z, other % nr)

    def group_from(k):
        return (o + no - k) % no

    o_copies = [
        pltpu.make_async_copy(o_hbm.at[c], o_buf.at[c], o_sem.at[c]) for c in range(2)
    ]
    for copy in o_copies:
        copy.start()

    barrier = pltpu.get_barrier_semaphore()

    def greet_group(k, carry):
        pl.semaphore_signal(barrier, inc=1, device_id=group(k)[1], device_id_type=MESH)
        return carry

    def greet_z(k, carry):
        pl.semaphore_signal(
            barrier, inc=1, device_id=(y * nz + (z + k) % nz, r), device_id_type=MESH
        )
        return carry

    lax.fori_loop(1, no, greet_group, 0)
    lax.fori_loop(1, nz, greet_z, 0)

    def block(yy, zz):
        return pl.ds(pl.multiple_of((yy * nz + zz) * lm, lm), lm)

    eye = one_hot((lm, lm), lambda i: i)
    for c in range(2):
        vg[c, block(y, z), :] = mm_nt(eye, v_ref[c]).astype(BF16)

    def operator_row(i):
        rr, rest = i // (ow * chunk), i % (ow * chunk)
        t, rest = rest // chunk, rest % chunk
        p, ii = rest // ni, rest % ni
        return (p * ow + t) * lm + rr * ni + ii

    width = min(256, modes)
    order = one_hot((rows, rows), operator_row)
    for c in range(2):
        o_copies[c].wait()

        def reorder(n, carry, c=c):
            columns = pl.ds(pl.multiple_of(n * width, width), width)
            o_buf[c, :, columns] = mm(order, o_buf[c, :, columns]).astype(BF16)
            return carry

        lax.fori_loop(0, modes // width, reorder, 0)

    pl.semaphore_wait(barrier, no - 1 + nz - 1)

    def send(src, dst, ssem, rsem, device):
        return pltpu.make_async_remote_copy(
            src_ref=src, dst_ref=dst, send_sem=ssem, recv_sem=rsem,
            device_id=device, device_id_type=MESH,
        )

    def y_first(d, yy):
        where = vg.at[0, block(yy, z)]
        return send(where, where, ys0.at[d - 1], yr0.at[d - 1], (((y + d) % ny) * nz + z, r))

    def ring0(way, k, d, incoming):
        yy = (y + ny - d) % ny
        if way == 0:
            zz = (z + 2 * nz - k - (1 if incoming else 0)) % nz
            to = right
        else:
            zz = (z + k + (1 if incoming else 0)) % nz
            to = left
        where = vg.at[0, block(yy, zz)]
        return send(where, where, zs0.at[way, k, d], zr0.at[way, k, d], (y * nz + to, r))

    def ring1(way, k, incoming):
        if way == 0:
            zz = (z + 2 * nz - k - (1 if incoming else 0)) % nz
            to = right
        else:
            zz = (z + k + (1 if incoming else 0)) % nz
            to = left
        where = vg.at[1, block(y, zz)]
        return send(where, where, zs1.at[way, k], zr1.at[way, k], (y * nz + to, r))

    def y_last(d, slot, zz, incoming):
        yy = (y + ny - d) % ny if incoming else y
        where = vg.at[1, block(yy, zz)]
        return send(
            where, where, ys1.at[d - 1, slot], yr1.at[d - 1, slot], (((y + d) % ny) * nz + z, r)
        )

    def slot_z(slot):
        return jnp.where(slot <= kr, z + nz - slot, z + slot - kr) % nz

    ways = ((0, kr), (1, kl))
    for d in range(1, ny):
        y_first(d, y).start()
    for way, steps in ways:
        if steps:
            ring0(way, 0, 0, False).start()
    for way, steps in ways:
        if steps:
            ring1(way, 0, False).start()
    for d in range(1, ny):
        y_last(d, 0, z, False).start()
    for d in range(1, ny):
        y_first(d, (y + ny - d) % ny).wait_recv()
        for way, steps in ways:
            if steps:
                ring0(way, 0, d, False).start()

    def ring_step(k, carry):
        for way, steps in ways:

            @pl.when(k < steps)
            def _(way=way, steps=steps):
                for d in range(ny):
                    ring0(way, k, d, True).wait_recv()

                    @pl.when(k + 1 < steps)
                    def _():
                        ring0(way, k + 1, d, False).start()

                ring1(way, k, True).wait_recv()

                @pl.when(k + 1 < steps)
                def _():
                    ring1(way, k + 1, False).start()

                slot = k + 1 + (kr if way else 0)
                zz = (z + 2 * nz - k - 1) % nz if way == 0 else (z + k + 1) % nz
                for d in range(1, ny):
                    y_last(d, slot, zz, False).start()

        return carry

    lax.fori_loop(0, kr, ring_step, 0)

    forward = one_hot((rank, rank), lambda i: (i % vw) * ow + i // vw)
    backward = one_hot((rank, rank), lambda i: (i % ow) * vw + i // ow)

    def exchange(c, d):
        to = (r + d) % nr
        return send(
            s_buf.at[c, to], x_buf.at[c, r], as_sem.at[c, d - 1], ar_sem.at[c, d - 1], (mode, to)
        )

    def exchange_from(c, d):
        source = (r + nr - d) % nr
        return send(
            s_buf.at[c, source], x_buf.at[c, source], as_sem.at[c, d - 1], ar_sem.at[c, d - 1],
            (mode, source),
        )

    def product(c):
        mt, nt = min(256, rows), min(256, ql * vw)

        def tile(n, carry):
            a = pl.ds(pl.multiple_of((n % (rows // mt)) * mt, mt), mt)
            b = pl.ds(pl.multiple_of((n // (rows // mt)) * nt, nt), nt)
            acc[a, b] = mm(o_buf[c, a, :], vg[c, :, b])
            return carry

        lax.fori_loop(0, (rows // mt) * (ql * vw // nt), tile, 0)

        def arrange(d, carry):
            to = (r + d) % nr
            base = to * (ow * chunk)
            for t in range(ow):
                strip = acc[pl.ds(pl.multiple_of(base + t * chunk, chunk), chunk), :].astype(BF16)
                for q in range(ql):
                    s_buf[c, to, q * chunk : (q + 1) * chunk, t * vw : (t + 1) * vw] = strip[
                        :, q * vw : (q + 1) * vw
                    ]

            @pl.when(d < nr)
            def _():
                exchange(c, d).start()

            return carry

        lax.fori_loop(1, nr + 1, arrange, 0)
        x_buf[c, r] = s_buf[c, r]

    def collect(c):
        def arrived(d, carry):
            exchange_from(c, d).wait_recv()
            return carry

        lax.fori_loop(1, nr, arrived, 0)
        per = ql * chunk
        lanes = min(128, rank)
        for source in range(nr):
            for h in range(rank // lanes):
                y_buf[h, source * per : (source + 1) * per, :] = x_buf[
                    c, source, :, h * lanes : (h + 1) * lanes
                ].astype(F32)
        bh, bl = split(b_ref[c + 1])
        for i in range(ni):
            raw = jnp.concatenate(
                [y_buf[h, pl.ds(i, rank, stride=ni), :] for h in range(rank // lanes)], axis=1
            ).astype(BF16)
            now = mm(raw, forward).astype(BF16)
            p_buf[i] = now
            pt_buf[i] = mm_nt(backward, raw).astype(BF16)
            q_out[c, i] = mm(now, bh) + mm(now, bl)

    def partial_gram(g):
        gh, gl = split(g)
        total = None
        for i in range(ni):
            now = p_buf[i]
            wh, wl = split(mm(gh, now) + mm(gl, now))
            flipped = pt_buf[i]
            term = mm(flipped, wh) + mm(flipped, wl)
            total = term if total is None else total + term
        part[...] = total * (1.0 / (modes * rank))

    def own_rows(index):
        return pl.ds(pl.multiple_of(index * rb_rows, rb_rows), rb_rows)

    def scatter(n, k):
        other, device = group(k)
        return send(part.at[own_rows(other)], ra.at[n, o], a_s.at[n, k - 1], a_r.at[n, k - 1], device)

    def along(n, k):
        return send(
            sb.at[n], rb.at[n, z], b_s.at[n, k - 1], b_r.at[n, k - 1],
            (y * nz + (z + k) % nz, r),
        )

    def spread(n, k):
        where = gram.at[n, own_rows(o)]
        return send(where, where, c_s.at[n, k - 1], c_r.at[n, k - 1], group(k)[1])

    def each(low, high, action):
        def body(k, carry):
            action(k)
            return carry

        lax.fori_loop(low, high, body, 0)

    def all_reduce(n):
        each(1, no, lambda k: scatter(n, k).start())
        ra[n, o] = part[own_rows(o), :]
        each(
            1, no,
            lambda k: send(
                ra.at[n, group_from(k)], ra.at[n, group_from(k)],
                a_s.at[n, k - 1], a_r.at[n, k - 1], group(k)[1],
            ).wait_recv(),
        )
        total = ra[n, 0]
        for k in range(1, no):
            total = total + ra[n, k]
        sb[n] = total
        rb[n, z] = total
        each(1, nz, lambda k: along(n, k).start())
        each(
            1, nz,
            lambda k: send(
                sb.at[n], rb.at[n, (z + nz - k) % nz], b_s.at[n, k - 1], b_r.at[n, k - 1],
                (y * nz + (z + k) % nz, r),
            ).wait_recv(),
        )
        total = rb[n, 0]
        for k in range(1, nz):
            total = total + rb[n, k]
        gram[n, own_rows(o), :] = total
        each(1, no, lambda k: spread(n, k).start())

        def landed(k):
            where = gram.at[n, own_rows(group_from(k))]
            send(where, where, c_s.at[n, k - 1], c_r.at[n, k - 1], group(k)[1]).wait_recv()

        each(1, no, landed)
        each(1, no, lambda k: scatter(n, k).wait_send())
        each(1, nz, lambda k: along(n, k).wait_send())
        each(1, no, lambda k: spread(n, k).wait_send())

    product(0)
    collect(0)
    partial_gram(g_ref[...])
    all_reduce(0)

    def y_arrived(slot):
        for d in range(1, ny):
            y_last(d, slot, slot_z(slot), True).wait_recv()

    each(0, nz, y_arrived)
    product(1)
    collect(1)
    partial_gram(gram[0])
    all_reduce(1)
    gram_out[...] = gram[...]

    for d in range(1, ny):
        y_first(d, y).wait_send()
    for way, steps in ways:
        if steps:

            def sent(k, way=way):
                for d in range(ny):
                    ring0(way, k, d, False).wait_send()
                ring1(way, k, False).wait_send()

            each(0, steps, sent)

    def y_sent(slot):
        for d in range(1, ny):
            y_last(d, slot, slot_z(slot), False).wait_send()

    each(0, nz, y_sent)
    for c in range(2):
        each(1, nr, lambda d, c=c: exchange(c, d).wait_send())


def shards(nr, nmode, operator_cores, vector_cores, left_gram, bases):
    cores, ow, _, lm, modes = operator_cores.shape
    ql, vw = vector_cores.shape[1:3]
    rank = left_gram.shape[0]
    ny = GRID_Y
    nz = nmode // ny
    ni = lm // nr
    rows = ow * ow * lm
    no = ny * nr
    rb_rows = rank // no
    kr = nz // 2
    dims = (ny, nz, nr, lm, ql, vw, ow, rank)
    dma = pltpu.SemaphoreType.DMA
    operator_rows = operator_cores.reshape(cores, rows, modes)
    vector_rows = vector_cores.reshape(cores, ql * vw, lm)
    vmem = pl.BlockSpec(memory_space=pltpu.VMEM)
    pieces, grams = pl.pallas_call(
        functools.partial(window_kernel, dims),
        out_shape=(
            jax.ShapeDtypeStruct((cores, ni, rank, bases.shape[2]), F32),
            jax.ShapeDtypeStruct((cores, rank, rank), F32),
        ),
        in_specs=[vmem, pl.BlockSpec(memory_space=pl.ANY), vmem, vmem],
        out_specs=(vmem, vmem),
        scratch_shapes=[
            pltpu.VMEM((cores, rows, modes), BF16),
            pltpu.VMEM((cores, modes, ql * vw), BF16),
            pltpu.VMEM((rows, ql * vw), F32),
            pltpu.VMEM((cores, nr, ql * ow * ni, rank), BF16),
            pltpu.VMEM((cores, nr, ql * ow * ni, rank), BF16),
            pltpu.VMEM((max(1, rank // 128), rank * ni, min(128, rank)), F32),
            pltpu.VMEM((ni, rank, rank), BF16),
            pltpu.VMEM((ni, rank, rank), BF16),
            pltpu.VMEM((rank, rank), F32),
            pltpu.VMEM((cores, no, rb_rows, rank), F32),
            pltpu.VMEM((cores, rb_rows, rank), F32),
            pltpu.VMEM((cores, nz, rb_rows, rank), F32),
            pltpu.VMEM((cores, rank, rank), F32),
            dma((2,)),
            dma((ny - 1,)), dma((ny - 1,)),
            dma((2, kr, ny)), dma((2, kr, ny)),
            dma((2, kr)), dma((2, kr)),
            dma((ny - 1, nz)), dma((ny - 1, nz)),
            dma((2, nr - 1)), dma((2, nr - 1)),
            dma((2, no - 1)), dma((2, no - 1)),
            dma((2, nz - 1)), dma((2, nz - 1)),
            dma((2, no - 1)), dma((2, no - 1)),
        ],
        compiler_params=pltpu.CompilerParams(collective_id=0, has_side_effects=True),
    )(vector_rows, operator_rows, left_gram, bases)
    results = []
    for core, gram_now in enumerate((left_gram, grams[0])):
        mixing = solve_mixing(gram_now, bases[core])
        results.append(
            jnp.einsum("ua,iav->uiv", mixing, pieces[core], precision=HIGHEST_PRECISION)
        )
    return (jnp.stack(results), grams[1])


def solution(mesh):
    placed = (P(None, None, None, "mode", None), P(None, "rank", None, "mode"), P(), P())
    return jax.shard_map(
        functools.partial(shards, mesh.shape["rank"], mesh.shape["mode"]),
        mesh=mesh,
        in_specs=placed,
        out_specs=(P(None, None, ("mode", "rank"), None), P()),
        check_vma=False,
    )
```

```python
import functools

import jax
import jax.numpy as jnp
from jax import lax
from jax.experimental import pallas as pl
from jax.experimental.pallas import tpu as pltpu
from jax.sharding import PartitionSpec as P

GRID_Y = 4
HIGHEST_PRECISION = lax.Precision.HIGHEST
MESH = pl.DeviceIdType.MESH
F32 = jnp.float32
BF16 = jnp.bfloat16


def mm(a, b):
    return jnp.dot(a, b, preferred_element_type=F32)


def mm_nt(a, b, precision=None):
    return lax.dot_general(
        a, b, (((1,), (1,)), ((), ())), precision=precision, preferred_element_type=F32
    )


def split(a):
    high = a.astype(BF16)
    return high, (a - high.astype(F32)).astype(BF16)


def one_hot(shape, target):
    rows = lax.broadcasted_iota(jnp.int32, shape, 0)
    columns = lax.broadcasted_iota(jnp.int32, shape, 1)
    return jnp.where(target(rows) == columns, 1.0, 0.0).astype(BF16)


def window_kernel(dims, *refs):
    (ny, nz, nr, lm, ql, vw, ow, rank) = dims
    (v_ref, o_hbm, g_ref, b_ref, r_out, gram_out,
     o_buf, vg, acc, s_buf, x_buf, y_buf, p_buf, pt_buf, q_buf, aug, part, ra, sb, rb, gram,
     o_sem, ys0, yr0, zs0, zr0, zs1, zr1, ys1, yr1, as_sem, ar_sem,
     a_s, a_r, b_s, b_r, c_s, c_r) = refs
    modes = ny * nz * lm
    ni = lm // nr
    rows = ow * ow * lm
    chunk = ow * ni
    no = ny * nr
    rb_rows = rank // no
    u_rank = b_ref.shape[1]
    head = aug.shape[1] - rank
    kr = nz // 2
    kl = nz - 1 - kr
    mode = lax.axis_index("mode")
    r = lax.axis_index("rank")
    y = mode // nz
    z = mode % nz
    o = y * nr + r
    right, left = (z + 1) % nz, (z + nz - 1) % nz

    def group(k):
        other = (o + k) % no
        return other, ((other // nr) * nz + z, other % nr)

    def group_from(k):
        return (o + no - k) % no

    o_copies = [
        pltpu.make_async_copy(o_hbm.at[c], o_buf.at[c], o_sem.at[c]) for c in range(2)
    ]
    for copy in o_copies:
        copy.start()

    barrier = pltpu.get_barrier_semaphore()

    def greet_group(k, carry):
        pl.semaphore_signal(barrier, inc=1, device_id=group(k)[1], device_id_type=MESH)
        return carry

    def greet_z(k, carry):
        pl.semaphore_signal(
            barrier, inc=1, device_id=(y * nz + (z + k) % nz, r), device_id_type=MESH
        )
        return carry

    lax.fori_loop(1, no, greet_group, 0)
    lax.fori_loop(1, nz, greet_z, 0)

    def block(yy, zz):
        return pl.ds(pl.multiple_of((yy * nz + zz) * lm, lm), lm)

    for c in range(2):
        for q in range(ql):
            vg[c, block(y, z), q * vw : (q + 1) * vw] = v_ref[c, q]

    def operator_row(i):
        rr, rest = i // (ow * chunk), i % (ow * chunk)
        t, rest = rest // chunk, rest % chunk
        p, ii = rest // ni, rest % ni
        return (p * ow + t) * lm + rr * ni + ii

    width = min(256, modes)
    order = one_hot((rows, rows), operator_row)
    for c in range(2):
        o_copies[c].wait()

        def reorder(n, carry, c=c):
            columns = pl.ds(pl.multiple_of(n * width, width), width)
            o_buf[c, :, columns] = mm(order, o_buf[c, :, columns]).astype(BF16)
            return carry

        lax.fori_loop(0, modes // width, reorder, 0)

    pl.semaphore_wait(barrier, no - 1 + nz - 1)

    def send(src, dst, ssem, rsem, device):
        return pltpu.make_async_remote_copy(
            src_ref=src, dst_ref=dst, send_sem=ssem, recv_sem=rsem,
            device_id=device, device_id_type=MESH,
        )

    def y_first(d, yy):
        where = vg.at[0, block(yy, z)]
        return send(where, where, ys0.at[d - 1], yr0.at[d - 1], (((y + d) % ny) * nz + z, r))

    def ring0(way, k, d, incoming):
        yy = (y + ny - d) % ny
        if way == 0:
            zz = (z + 2 * nz - k - (1 if incoming else 0)) % nz
            to = right
        else:
            zz = (z + k + (1 if incoming else 0)) % nz
            to = left
        where = vg.at[0, block(yy, zz)]
        return send(where, where, zs0.at[way, k, d], zr0.at[way, k, d], (y * nz + to, r))

    def ring1(way, k, incoming):
        if way == 0:
            zz = (z + 2 * nz - k - (1 if incoming else 0)) % nz
            to = right
        else:
            zz = (z + k + (1 if incoming else 0)) % nz
            to = left
        where = vg.at[1, block(y, zz)]
        return send(where, where, zs1.at[way, k], zr1.at[way, k], (y * nz + to, r))

    def y_last(d, slot, zz, incoming):
        yy = (y + ny - d) % ny if incoming else y
        where = vg.at[1, block(yy, zz)]
        return send(
            where, where, ys1.at[d - 1, slot], yr1.at[d - 1, slot], (((y + d) % ny) * nz + z, r)
        )

    def slot_z(slot):
        return jnp.where(slot <= kr, z + nz - slot, z + slot - kr) % nz

    ways = ((0, kr), (1, kl))
    for d in range(1, ny):
        y_first(d, y).start()
    for way, steps in ways:
        if steps:
            ring0(way, 0, 0, False).start()
    for way, steps in ways:
        if steps:
            ring1(way, 0, False).start()
    for d in range(1, ny):
        y_last(d, 0, z, False).start()
    for d in range(1, ny):
        y_first(d, (y + ny - d) % ny).wait_recv()
        for way, steps in ways:
            if steps:
                ring0(way, 0, d, False).start()

    def ring_step(k, carry):
        for way, steps in ways:

            @pl.when(k < steps)
            def _(way=way, steps=steps):
                for d in range(ny):
                    ring0(way, k, d, True).wait_recv()

                    @pl.when(k + 1 < steps)
                    def _():
                        ring0(way, k + 1, d, False).start()

                ring1(way, k, True).wait_recv()

                @pl.when(k + 1 < steps)
                def _():
                    ring1(way, k + 1, False).start()

                slot = k + 1 + (kr if way else 0)
                zz = (z + 2 * nz - k - 1) % nz if way == 0 else (z + k + 1) % nz
                for d in range(1, ny):
                    y_last(d, slot, zz, False).start()

        return carry

    lax.fori_loop(0, kr, ring_step, 0)

    forward = one_hot((rank, rank), lambda i: (i % vw) * ow + i // vw)
    backward = one_hot((rank, rank), lambda i: (i % ow) * vw + i // ow)

    def exchange(c, d):
        to = (r + d) % nr
        return send(
            s_buf.at[c, to], x_buf.at[c, r], as_sem.at[c, d - 1], ar_sem.at[c, d - 1], (mode, to)
        )

    def exchange_from(c, d):
        source = (r + nr - d) % nr
        return send(
            s_buf.at[c, source], x_buf.at[c, source], as_sem.at[c, d - 1], ar_sem.at[c, d - 1],
            (mode, source),
        )

    def product(c):
        mt, nt = min(256, rows), min(256, ql * vw)

        def tile(n, carry):
            a = pl.ds(pl.multiple_of((n % (rows // mt)) * mt, mt), mt)
            b = pl.ds(pl.multiple_of((n // (rows // mt)) * nt, nt), nt)
            acc[a, b] = mm(o_buf[c, a, :], vg[c, :, b])
            return carry

        lax.fori_loop(0, (rows // mt) * (ql * vw // nt), tile, 0)

        def arrange(d, carry):
            to = (r + d) % nr
            base = to * (ow * chunk)
            for t in range(ow):
                strip = acc[pl.ds(pl.multiple_of(base + t * chunk, chunk), chunk), :].astype(BF16)
                for q in range(ql):
                    s_buf[c, to, q * chunk : (q + 1) * chunk, t * vw : (t + 1) * vw] = strip[
                        :, q * vw : (q + 1) * vw
                    ]

            @pl.when(d < nr)
            def _():
                exchange(c, d).start()

            return carry

        lax.fori_loop(1, nr + 1, arrange, 0)
        x_buf[c, r] = s_buf[c, r]

    def collect(c):
        def arrived(d, carry):
            exchange_from(c, d).wait_recv()
            return carry

        lax.fori_loop(1, nr, arrived, 0)
        per = ql * chunk
        lanes = min(128, rank)
        for source in range(nr):
            for h in range(rank // lanes):
                y_buf[h, source * per : (source + 1) * per, :] = x_buf[
                    c, source, :, h * lanes : (h + 1) * lanes
                ].astype(F32)
        bh, bl = split(b_ref[c + 1])
        for i in range(ni):
            raw = jnp.concatenate(
                [y_buf[h, pl.ds(i, rank, stride=ni), :] for h in range(rank // lanes)], axis=1
            ).astype(BF16)
            now = mm(raw, forward).astype(BF16)
            p_buf[i] = now
            pt_buf[i] = mm_nt(backward, raw).astype(BF16)
            q_buf[c, :, i * u_rank : (i + 1) * u_rank] = mm_nt(now, bh) + mm_nt(now, bl)

    def partial_gram(g):
        gh, gl = split(g)
        total = None
        for i in range(ni):
            now = p_buf[i]
            wh, wl = split(mm(gh, now) + mm(gl, now))
            flipped = pt_buf[i]
            term = mm(flipped, wh) + mm(flipped, wl)
            total = term if total is None else total + term
        part[...] = total * (1.0 / (modes * rank))

    def own_rows(index):
        return pl.ds(pl.multiple_of(index * rb_rows, rb_rows), rb_rows)

    def scatter(n, k):
        other, device = group(k)
        return send(part.at[own_rows(other)], ra.at[n, o], a_s.at[n, k - 1], a_r.at[n, k - 1], device)

    def along(n, k):
        return send(
            sb.at[n], rb.at[n, z], b_s.at[n, k - 1], b_r.at[n, k - 1],
            (y * nz + (z + k) % nz, r),
        )

    def spread(n, k):
        where = gram.at[n, own_rows(o)]
        return send(where, where, c_s.at[n, k - 1], c_r.at[n, k - 1], group(k)[1])

    def each(low, high, action):
        def body(k, carry):
            action(k)
            return carry

        lax.fori_loop(low, high, body, 0)

    def solve_start(c, g):
        basis = b_ref[c]
        projected = jnp.dot(
            basis, g, precision=HIGHEST_PRECISION, preferred_element_type=F32
        )
        reduced = mm_nt(projected, basis, HIGHEST_PRECISION)
        aug[:, :head] = jnp.zeros((u_rank, head), F32)
        aug[:, :u_rank] = 0.5 * (reduced + reduced.T)
        aug[:, head:] = projected

    def solve_steps(low, high):
        row_index = lax.broadcasted_iota(jnp.int32, (u_rank, 1), 0)
        lane_index = lax.broadcasted_iota(jnp.int32, (u_rank, head), 1)

        def step(k):
            row = aug[pl.ds(k, 1), :]
            chosen = lane_index == k
            column = jnp.sum(
                jnp.where(chosen, aug[:, :head], 0.0), axis=1, keepdims=True
            )
            pivot = jnp.sum(
                jnp.where(chosen[:1], row[:, :head], 0.0), axis=1, keepdims=True
            )
            scaled = row / pivot
            aug[...] = aug[...] - jnp.where(row_index == k, 0.0, column) * scaled
            aug[pl.ds(k, 1), :] = scaled

        each(low, high, step)

    def solve_end(c):
        mh, ml = split(aug[:, head:])
        for i in range(ni):
            qh, ql_ = split(q_buf[c, :, i * u_rank : (i + 1) * u_rank])
            r_out[c, i] = mm(mh, qh) + (mm(mh, ql_) + mm(ml, qh))

    def all_reduce(n, g):
        each(1, no, lambda k: scatter(n, k).start())
        solve_start(n, g)
        solve_steps(0, u_rank // 4)
        ra[n, o] = part[own_rows(o), :]
        each(
            1, no,
            lambda k: send(
                ra.at[n, group_from(k)], ra.at[n, group_from(k)],
                a_s.at[n, k - 1], a_r.at[n, k - 1], group(k)[1],
            ).wait_recv(),
        )
        total = ra[n, 0]
        for k in range(1, no):
            total = total + ra[n, k]
        sb[n] = total
        rb[n, z] = total
        each(1, nz, lambda k: along(n, k).start())
        solve_steps(u_rank // 4, u_rank)
        each(
            1, nz,
            lambda k: send(
                sb.at[n], rb.at[n, (z + nz - k) % nz], b_s.at[n, k - 1], b_r.at[n, k - 1],
                (y * nz + (z + k) % nz, r),
            ).wait_recv(),
        )
        total = rb[n, 0]
        for k in range(1, nz):
            total = total + rb[n, k]
        gram[n, own_rows(o), :] = total
        each(1, no, lambda k: spread(n, k).start())
        solve_end(n)

        def landed(k):
            where = gram.at[n, own_rows(group_from(k))]
            send(where, where, c_s.at[n, k - 1], c_r.at[n, k - 1], group(k)[1]).wait_recv()

        each(1, no, landed)
        each(1, no, lambda k: scatter(n, k).wait_send())
        each(1, nz, lambda k: along(n, k).wait_send())
        each(1, no, lambda k: spread(n, k).wait_send())

    product(0)
    collect(0)
    partial_gram(g_ref[...])
    all_reduce(0, g_ref[...])

    def y_arrived(slot):
        for d in range(1, ny):
            y_last(d, slot, slot_z(slot), True).wait_recv()

    each(0, nz, y_arrived)
    product(1)
    collect(1)
    partial_gram(gram[0])
    all_reduce(1, gram[0])
    gram_out[...] = gram[1]

    for d in range(1, ny):
        y_first(d, y).wait_send()
    for way, steps in ways:
        if steps:

            def sent(k, way=way):
                for d in range(ny):
                    ring0(way, k, d, False).wait_send()
                ring1(way, k, False).wait_send()

            each(0, steps, sent)

    def y_sent(slot):
        for d in range(1, ny):
            y_last(d, slot, slot_z(slot), False).wait_send()

    each(0, nz, y_sent)
    for c in range(2):
        each(1, nr, lambda d, c=c: exchange(c, d).wait_send())


def shards(nr, nmode, operator_cores, vector_cores, left_gram, bases):
    cores, ow, _, lm, modes = operator_cores.shape
    ql, vw = vector_cores.shape[1:3]
    rank = left_gram.shape[0]
    ny = GRID_Y
    nz = nmode // ny
    ni = lm // nr
    rows = ow * ow * lm
    no = ny * nr
    rb_rows = rank // no
    kr = nz // 2
    dims = (ny, nz, nr, lm, ql, vw, ow, rank)
    dma = pltpu.SemaphoreType.DMA
    operator_rows = operator_cores.reshape(cores, rows, modes)
    vector_rows = vector_cores.transpose(0, 1, 3, 2)
    bases_rows = bases.transpose(0, 2, 1)
    out_rank = bases.shape[2]
    vmem = pl.BlockSpec(memory_space=pltpu.VMEM)
    pieces, gram = pl.pallas_call(
        functools.partial(window_kernel, dims),
        out_shape=(
            jax.ShapeDtypeStruct((cores, ni, out_rank, out_rank), F32),
            jax.ShapeDtypeStruct((rank, rank), F32),
        ),
        in_specs=[vmem, pl.BlockSpec(memory_space=pl.ANY), vmem, vmem],
        out_specs=(vmem, vmem),
        scratch_shapes=[
            pltpu.VMEM((cores, rows, modes), BF16),
            pltpu.VMEM((cores, modes, ql * vw), BF16),
            pltpu.VMEM((rows, ql * vw), F32),
            pltpu.VMEM((cores, nr, ql * ow * ni, rank), BF16),
            pltpu.VMEM((cores, nr, ql * ow * ni, rank), BF16),
            pltpu.VMEM((max(1, rank // 128), rank * ni, min(128, rank)), F32),
            pltpu.VMEM((ni, rank, rank), BF16),
            pltpu.VMEM((ni, rank, rank), BF16),
            pltpu.VMEM((cores, rank, ni * out_rank), F32),
            pltpu.VMEM((out_rank, 128 + rank), F32),
            pltpu.VMEM((rank, rank), F32),
            pltpu.VMEM((cores, no, rb_rows, rank), F32),
            pltpu.VMEM((cores, rb_rows, rank), F32),
            pltpu.VMEM((cores, nz, rb_rows, rank), F32),
            pltpu.VMEM((cores, rank, rank), F32),
            dma((2,)),
            dma((ny - 1,)), dma((ny - 1,)),
            dma((2, kr, ny)), dma((2, kr, ny)),
            dma((2, kr)), dma((2, kr)),
            dma((ny - 1, nz)), dma((ny - 1, nz)),
            dma((2, nr - 1)), dma((2, nr - 1)),
            dma((2, no - 1)), dma((2, no - 1)),
            dma((2, nz - 1)), dma((2, nz - 1)),
            dma((2, no - 1)), dma((2, no - 1)),
        ],
        compiler_params=pltpu.CompilerParams(collective_id=0, has_side_effects=True),
    )(vector_rows, operator_rows, left_gram, bases_rows)
    return (pieces.transpose(0, 2, 1, 3), gram)


def solution(mesh):
    placed = (P(None, None, None, "mode", None), P(None, "rank", None, "mode"), P(), P())
    return jax.shard_map(
        functools.partial(shards, mesh.shape["rank"], mesh.shape["mode"]),
        mesh=mesh,
        in_specs=placed,
        out_specs=(P(None, None, ("mode", "rank"), None), P()),
        check_vma=False,
    )
```

```python
import functools

import jax
import jax.numpy as jnp
from jax import lax
from jax.experimental import pallas as pl
from jax.experimental.pallas import tpu as pltpu
from jax.sharding import PartitionSpec as P

GRID_Y = 4
HIGHEST_PRECISION = lax.Precision.HIGHEST
MESH = pl.DeviceIdType.MESH
F32 = jnp.float32
BF16 = jnp.bfloat16


def mm(a, b):
    return jnp.dot(a, b, preferred_element_type=F32)


def mm_nt(a, b, precision=None):
    return lax.dot_general(
        a, b, (((1,), (1,)), ((), ())), precision=precision, preferred_element_type=F32
    )


def split(a):
    high = a.astype(BF16)
    return high, (a - high.astype(F32)).astype(BF16)


def one_hot(shape, target):
    rows = lax.broadcasted_iota(jnp.int32, shape, 0)
    columns = lax.broadcasted_iota(jnp.int32, shape, 1)
    return jnp.where(target(rows) == columns, 1.0, 0.0).astype(BF16)


def window_kernel(dims, *refs):
    (ny, nz, nr, lm, ql, vw, ow, rank) = dims
    (v_ref, o_hbm, g_ref, b_ref, r_out, gram_out,
     o_buf, vg, acc, s_buf, x_buf, y_buf, p_buf, pt_buf, q_buf, aug, part, ra, sb, rb, gram,
     o_sem, ys0, yr0, zs0, zr0, zs1, zr1, ys1, yr1, as_sem, ar_sem,
     a_s, a_r, b_s, b_r, c_s, c_r) = refs
    modes = ny * nz * lm
    ni = lm // nr
    rows = ow * ow * lm
    chunk = ow * ni
    no = ny * nr
    rb_rows = rank // no
    u_rank = b_ref.shape[1]
    head = aug.shape[1] - rank
    cut = ql * vw // 4
    kr = nz // 2
    kl = nz - 1 - kr
    mode = lax.axis_index("mode")
    r = lax.axis_index("rank")
    y = mode // nz
    z = mode % nz
    o = y * nr + r
    right, left = (z + 1) % nz, (z + nz - 1) % nz

    def group(k):
        other = (o + k) % no
        return other, ((other // nr) * nz + z, other % nr)

    def group_from(k):
        return (o + no - k) % no

    o_copies = [
        pltpu.make_async_copy(o_hbm.at[c], o_buf.at[c], o_sem.at[c]) for c in range(2)
    ]
    for copy in o_copies:
        copy.start()

    barrier = pltpu.get_barrier_semaphore()

    def greet_group(k, carry):
        pl.semaphore_signal(barrier, inc=1, device_id=group(k)[1], device_id_type=MESH)
        return carry

    def greet_z(k, carry):
        pl.semaphore_signal(
            barrier, inc=1, device_id=(y * nz + (z + k) % nz, r), device_id_type=MESH
        )
        return carry

    lax.fori_loop(1, no, greet_group, 0)
    lax.fori_loop(1, nz, greet_z, 0)

    def block(yy, zz):
        return pl.ds(pl.multiple_of((yy * nz + zz) * lm, lm), lm)

    for c in range(2):
        for q in range(ql):
            vg[c, block(y, z), q * vw : (q + 1) * vw] = v_ref[c, q]

    def operator_row(i):
        rr, rest = i // (ow * chunk), i % (ow * chunk)
        t, rest = rest // chunk, rest % chunk
        p, ii = rest // ni, rest % ni
        return (p * ow + t) * lm + rr * ni + ii

    width = min(256, modes)
    order = one_hot((rows, rows), operator_row)
    for c in range(2):
        o_copies[c].wait()

        def reorder(n, carry, c=c):
            columns = pl.ds(pl.multiple_of(n * width, width), width)
            o_buf[c, :, columns] = mm(order, o_buf[c, :, columns]).astype(BF16)
            return carry

        lax.fori_loop(0, modes // width, reorder, 0)

    pl.semaphore_wait(barrier, no - 1 + nz - 1)

    def send(src, dst, ssem, rsem, device):
        return pltpu.make_async_remote_copy(
            src_ref=src, dst_ref=dst, send_sem=ssem, recv_sem=rsem,
            device_id=device, device_id_type=MESH,
        )

    def y_first(d, yy):
        where = vg.at[0, block(yy, z), :cut]
        return send(where, where, ys0.at[d - 1], yr0.at[d - 1], (((y + d) % ny) * nz + z, r))

    def towards(way, k, incoming):
        ahead = 1 if incoming else 0
        if way == 0:
            return (z + 2 * nz - k - ahead) % nz, right
        return (z + k + ahead) % nz, left

    def ring0(way, k, d, incoming):
        zz, to = towards(way, k, incoming)
        where = vg.at[0, block((y + ny - d) % ny, zz), :cut]
        return send(where, where, zs0.at[way, k, d], zr0.at[way, k, d], (y * nz + to, r))

    def part_of(c, yy, zz):
        if c == 0:
            return vg.at[0, block(yy, zz), cut:]
        return vg.at[1, block(yy, zz)]

    def ring1(c, way, k, incoming):
        zz, to = towards(way, k, incoming)
        where = part_of(c, y, zz)
        return send(where, where, zs1.at[c, way, k], zr1.at[c, way, k], (y * nz + to, r))

    def y_last(c, d, slot, zz, incoming):
        where = part_of(c, (y + ny - d) % ny if incoming else y, zz)
        return send(
            where, where, ys1.at[c, d - 1, slot], yr1.at[c, d - 1, slot],
            (((y + d) % ny) * nz + z, r),
        )

    def slot_z(slot):
        return jnp.where(slot <= kr, z + nz - slot, z + slot - kr) % nz

    ways = tuple((way, steps) for way, steps in ((0, kr), (1, kl)) if steps)
    for way, steps in ways:
        ring1(0, way, 0, False).start()
    for d in range(1, ny):
        y_first(d, y).start()
    for way, steps in ways:
        ring0(way, 0, 0, False).start()
    for d in range(1, ny):
        y_last(0, d, 0, z, False).start()
    for way, steps in ways:
        ring1(1, way, 0, False).start()
    for d in range(1, ny):
        y_first(d, (y + ny - d) % ny).wait_recv()
        for way, steps in ways:
            ring0(way, 0, d, False).start()

    def ring_step(k, carry):
        for way, steps in ways:

            @pl.when(k < steps)
            def _(way=way, steps=steps):
                ring1(0, way, k, True).wait_recv()

                @pl.when(k + 1 < steps)
                def _():
                    ring1(0, way, k + 1, False).start()

                for d in range(1, ny):
                    y_last(0, d, k + 1 + (kr if way else 0), towards(way, k, True)[0], False).start()

        for way, steps in ways:

            @pl.when(k < steps)
            def _(way=way, steps=steps):
                for d in range(ny):
                    ring0(way, k, d, True).wait_recv()

                    @pl.when(k + 1 < steps)
                    def _():
                        ring0(way, k + 1, d, False).start()

                ring1(1, way, k, True).wait_recv()

                @pl.when(k + 1 < steps)
                def _():
                    ring1(1, way, k + 1, False).start()

        return carry

    lax.fori_loop(0, kr, ring_step, 0)

    def y_arrived(c, slot):
        for d in range(1, ny):
            y_last(c, d, slot, slot_z(slot), True).wait_recv()

    def y_pass(slot):
        for d in range(1, ny):
            y_last(1, d, slot, slot_z(slot), False).start()

    def each(low, high, action):
        def body(k, carry):
            action(k)
            return carry

        lax.fori_loop(low, high, body, 0)

    each(0, nz, functools.partial(y_arrived, 0))
    each(0, nz, y_pass)

    forward = one_hot((rank, rank), lambda i: (i % vw) * ow + i // vw)
    backward = one_hot((rank, rank), lambda i: (i % ow) * vw + i // ow)

    def exchange(c, d):
        to = (r + d) % nr
        return send(
            s_buf.at[c, to], x_buf.at[c, r], as_sem.at[c, d - 1], ar_sem.at[c, d - 1], (mode, to)
        )

    def exchange_from(c, d):
        source = (r + nr - d) % nr
        return send(
            s_buf.at[c, source], x_buf.at[c, source], as_sem.at[c, d - 1], ar_sem.at[c, d - 1],
            (mode, source),
        )

    def product(c):
        mt, nt = min(256, rows), min(256, ql * vw)

        def tile(n, carry):
            a = pl.ds(pl.multiple_of((n % (rows // mt)) * mt, mt), mt)
            b = pl.ds(pl.multiple_of((n // (rows // mt)) * nt, nt), nt)
            acc[a, b] = mm(o_buf[c, a, :], vg[c, :, b])
            return carry

        lax.fori_loop(0, (rows // mt) * (ql * vw // nt), tile, 0)

        def arrange(d, carry):
            to = (r + d) % nr
            base = to * (ow * chunk)
            for t in range(ow):
                strip = acc[pl.ds(pl.multiple_of(base + t * chunk, chunk), chunk), :].astype(BF16)
                for q in range(ql):
                    s_buf[c, to, q * chunk : (q + 1) * chunk, t * vw : (t + 1) * vw] = strip[
                        :, q * vw : (q + 1) * vw
                    ]

            @pl.when(d < nr)
            def _():
                exchange(c, d).start()

            return carry

        lax.fori_loop(1, nr + 1, arrange, 0)
        x_buf[c, r] = s_buf[c, r]

    def collect(c):
        def arrived(d, carry):
            exchange_from(c, d).wait_recv()
            return carry

        lax.fori_loop(1, nr, arrived, 0)
        per = ql * chunk
        lanes = min(128, rank)
        for source in range(nr):
            for h in range(rank // lanes):
                y_buf[h, source * per : (source + 1) * per, :] = x_buf[
                    c, source, :, h * lanes : (h + 1) * lanes
                ].astype(F32)
        bh, bl = split(b_ref[c + 1])
        for i in range(ni):
            raw = jnp.concatenate(
                [y_buf[h, pl.ds(i, rank, stride=ni), :] for h in range(rank // lanes)], axis=1
            ).astype(BF16)
            now = mm(raw, forward).astype(BF16)
            p_buf[i] = now
            pt_buf[i] = mm_nt(backward, raw).astype(BF16)
            q_buf[c, :, i * u_rank : (i + 1) * u_rank] = mm_nt(now, bh) + mm_nt(now, bl)

    def partial_gram(g):
        gh, gl = split(g)
        total = None
        for i in range(ni):
            now = p_buf[i]
            wh, wl = split(mm(gh, now) + mm(gl, now))
            flipped = pt_buf[i]
            term = mm(flipped, wh) + mm(flipped, wl)
            total = term if total is None else total + term
        part[...] = total * (1.0 / (modes * rank))

    def own_rows(index):
        return pl.ds(pl.multiple_of(index * rb_rows, rb_rows), rb_rows)

    def scatter(n, k):
        other, device = group(k)
        return send(part.at[own_rows(other)], ra.at[n, o], a_s.at[n, k - 1], a_r.at[n, k - 1], device)

    def along(n, k):
        return send(
            sb.at[n], rb.at[n, z], b_s.at[n, k - 1], b_r.at[n, k - 1],
            (y * nz + (z + k) % nz, r),
        )

    def spread(n, k):
        where = gram.at[n, own_rows(o)]
        return send(where, where, c_s.at[n, k - 1], c_r.at[n, k - 1], group(k)[1])

    def solve_start(c, g):
        basis = b_ref[c]
        projected = jnp.dot(
            basis, g, precision=HIGHEST_PRECISION, preferred_element_type=F32
        )
        reduced = mm_nt(projected, basis, HIGHEST_PRECISION)
        aug[:, :head] = jnp.zeros((u_rank, head), F32)
        aug[:, :u_rank] = 0.5 * (reduced + reduced.T)
        aug[:, head:] = projected

    def solve_steps(low, high):
        row_index = lax.broadcasted_iota(jnp.int32, (u_rank, 1), 0)
        lane_index = lax.broadcasted_iota(jnp.int32, (u_rank, head), 1)

        def step(k):
            row = aug[pl.ds(k, 1), :]
            chosen = lane_index == k
            column = jnp.sum(
                jnp.where(chosen, aug[:, :head], 0.0), axis=1, keepdims=True
            )
            pivot = jnp.sum(
                jnp.where(chosen[:1], row[:, :head], 0.0), axis=1, keepdims=True
            )
            scaled = row / pivot
            aug[...] = aug[...] - jnp.where(row_index == k, 0.0, column) * scaled
            aug[pl.ds(k, 1), :] = scaled

        each(low, high, step)

    def solve_end(c):
        mh, ml = split(aug[:, head:])
        for i in range(ni):
            qh, ql_ = split(q_buf[c, :, i * u_rank : (i + 1) * u_rank])
            r_out[c, :, i, :] = mm(mh, qh) + (mm(mh, ql_) + mm(ml, qh))

    def all_reduce(n, fill_a, fill_b, fill_c):
        each(1, no, lambda k: scatter(n, k).start())
        fill_a()
        ra[n, o] = part[own_rows(o), :]
        each(
            1, no,
            lambda k: send(
                ra.at[n, group_from(k)], ra.at[n, group_from(k)],
                a_s.at[n, k - 1], a_r.at[n, k - 1], group(k)[1],
            ).wait_recv(),
        )
        total = ra[n, 0]
        for k in range(1, no):
            total = total + ra[n, k]
        sb[n] = total
        rb[n, z] = total
        each(1, nz, lambda k: along(n, k).start())
        fill_b()
        each(
            1, nz,
            lambda k: send(
                sb.at[n], rb.at[n, (z + nz - k) % nz], b_s.at[n, k - 1], b_r.at[n, k - 1],
                (y * nz + (z + k) % nz, r),
            ).wait_recv(),
        )
        total = rb[n, 0]
        for k in range(1, nz):
            total = total + rb[n, k]
        gram[n, own_rows(o), :] = total
        each(1, no, lambda k: spread(n, k).start())
        fill_c()

        def landed(k):
            where = gram.at[n, own_rows(group_from(k))]
            send(where, where, c_s.at[n, k - 1], c_r.at[n, k - 1], group(k)[1]).wait_recv()

        each(1, no, landed)
        each(1, no, lambda k: scatter(n, k).wait_send())
        each(1, nz, lambda k: along(n, k).wait_send())
        each(1, no, lambda k: spread(n, k).wait_send())

    def solve_first():
        solve_start(0, g_ref[...])
        solve_steps(0, u_rank)
        solve_end(0)

    def product_second():
        each(0, nz, functools.partial(y_arrived, 1))
        product(1)

    def solve_second():
        solve_start(1, gram[0])
        solve_steps(0, u_rank // 4)

    product(0)
    collect(0)
    partial_gram(g_ref[...])
    all_reduce(0, solve_first, product_second, lambda: collect(1))
    partial_gram(gram[0])
    all_reduce(
        1, solve_second, lambda: solve_steps(u_rank // 4, u_rank), lambda: solve_end(1)
    )
    gram_out[...] = gram[1]

    for d in range(1, ny):
        y_first(d, y).wait_send()
    for way, steps in ways:

        def sent(k, way=way):
            for d in range(ny):
                ring0(way, k, d, False).wait_send()
            for c in range(2):
                ring1(c, way, k, False).wait_send()

        each(0, steps, sent)

    def y_sent(slot):
        for c in range(2):
            for d in range(1, ny):
                y_last(c, d, slot, slot_z(slot), False).wait_send()

    each(0, nz, y_sent)
    for c in range(2):
        each(1, nr, lambda d, c=c: exchange(c, d).wait_send())


def shards(nr, nmode, operator_cores, vector_cores, left_gram, bases):
    cores, ow, _, lm, modes = operator_cores.shape
    ql, vw = vector_cores.shape[1:3]
    rank = left_gram.shape[0]
    ny = GRID_Y
    nz = nmode // ny
    ni = lm // nr
    rows = ow * ow * lm
    no = ny * nr
    rb_rows = rank // no
    kr = nz // 2
    dims = (ny, nz, nr, lm, ql, vw, ow, rank)
    dma = pltpu.SemaphoreType.DMA
    operator_rows = operator_cores.reshape(cores, rows, modes)
    vector_rows = vector_cores.transpose(0, 1, 3, 2)
    bases_rows = bases.transpose(0, 2, 1)
    out_rank = bases.shape[2]
    vmem = pl.BlockSpec(memory_space=pltpu.VMEM)
    pieces, gram = pl.pallas_call(
        functools.partial(window_kernel, dims),
        out_shape=(
            jax.ShapeDtypeStruct((cores, out_rank, ni, out_rank), F32),
            jax.ShapeDtypeStruct((rank, rank), F32),
        ),
        in_specs=[vmem, pl.BlockSpec(memory_space=pl.ANY), vmem, vmem],
        out_specs=(vmem, vmem),
        scratch_shapes=[
            pltpu.VMEM((cores, rows, modes), BF16),
            pltpu.VMEM((cores, modes, ql * vw), BF16),
            pltpu.VMEM((rows, ql * vw), F32),
            pltpu.VMEM((cores, nr, ql * ow * ni, rank), BF16),
            pltpu.VMEM((cores, nr, ql * ow * ni, rank), BF16),
            pltpu.VMEM((max(1, rank // 128), rank * ni, min(128, rank)), F32),
            pltpu.VMEM((ni, rank, rank), BF16),
            pltpu.VMEM((ni, rank, rank), BF16),
            pltpu.VMEM((cores, rank, ni * out_rank), F32),
            pltpu.VMEM((out_rank, 128 + rank), F32),
            pltpu.VMEM((rank, rank), F32),
            pltpu.VMEM((cores, no, rb_rows, rank), F32),
            pltpu.VMEM((cores, rb_rows, rank), F32),
            pltpu.VMEM((cores, nz, rb_rows, rank), F32),
            pltpu.VMEM((cores, rank, rank), F32),
            dma((2,)),
            dma((ny - 1,)), dma((ny - 1,)),
            dma((2, kr, ny)), dma((2, kr, ny)),
            dma((2, 2, kr)), dma((2, 2, kr)),
            dma((2, ny - 1, nz)), dma((2, ny - 1, nz)),
            dma((2, nr - 1)), dma((2, nr - 1)),
            dma((2, no - 1)), dma((2, no - 1)),
            dma((2, nz - 1)), dma((2, nz - 1)),
            dma((2, no - 1)), dma((2, no - 1)),
        ],
        compiler_params=pltpu.CompilerParams(collective_id=0, has_side_effects=True),
    )(vector_rows, operator_rows, left_gram, bases_rows)
    return pieces, gram


def solution(mesh):
    placed = (P(None, None, None, "mode", None), P(None, "rank", None, "mode"), P(), P())
    return jax.shard_map(
        functools.partial(shards, mesh.shape["rank"], mesh.shape["mode"]),
        mesh=mesh,
        in_specs=placed,
        out_specs=(P(None, None, ("mode", "rank"), None), P()),
        check_vma=False,
    )
```

```python
import functools

import jax
import jax.numpy as jnp
from jax import lax
from jax.experimental import pallas as pl
from jax.experimental.pallas import tpu as pltpu
from jax.sharding import PartitionSpec as P

GRID_Y = 4
HIGHEST_PRECISION = lax.Precision.HIGHEST
MESH = pl.DeviceIdType.MESH
F32 = jnp.float32
BF16 = jnp.bfloat16


def mm(a, b):
    return jnp.dot(a, b, preferred_element_type=F32)


def mm_nt(a, b, precision=None):
    return lax.dot_general(
        a, b, (((1,), (1,)), ((), ())), precision=precision, preferred_element_type=F32
    )


def split(a):
    high = a.astype(BF16)
    return high, (a - high.astype(F32)).astype(BF16)


def one_hot(shape, target):
    rows = lax.broadcasted_iota(jnp.int32, shape, 0)
    columns = lax.broadcasted_iota(jnp.int32, shape, 1)
    return jnp.where(target(rows) == columns, 1.0, 0.0).astype(BF16)


def window_kernel(dims, *refs):
    (ny, nz, nr, lm, ql, vw, ow, rank) = dims
    (v_ref, o_hbm, g_ref, b_ref, r_out, gram_out,
     o_buf, vg, acc, s_buf, x_buf, y_buf, p_buf, pt_buf, q_buf, aug, part, ra, sb, rb, gram,
     o_sem, ys0, yr0, zs0, zr0, zs1, zr1, ys1, yr1, as_sem, ar_sem,
     a_s, a_r, b_s, b_r, c_s, c_r) = refs
    modes = ny * nz * lm
    ni = lm // nr
    rows = ow * ow * lm
    chunk = ow * ni
    no = ny * nr
    rb_rows = rank // no
    u_rank = b_ref.shape[1]
    head = aug.shape[1] - rank
    cut = ql * vw // 4
    kr = nz // 2
    kl = nz - 1 - kr
    direct = (1, ny - 1)
    mode = lax.axis_index("mode")
    r = lax.axis_index("rank")
    y = mode // nz
    z = mode % nz
    o = y * nr + r
    right, left = (z + 1) % nz, (z + nz - 1) % nz

    def group(k):
        other = (o + k) % no
        return other, ((other // nr) * nz + z, other % nr)

    def group_from(k):
        return (o + no - k) % no

    o_copies = [
        pltpu.make_async_copy(o_hbm.at[c], o_buf.at[c], o_sem.at[c]) for c in range(2)
    ]
    for copy in o_copies:
        copy.start()

    barrier = pltpu.get_barrier_semaphore()

    def greet_group(k, carry):
        pl.semaphore_signal(barrier, inc=1, device_id=group(k)[1], device_id_type=MESH)
        return carry

    def greet_z(k, carry):
        pl.semaphore_signal(
            barrier, inc=1, device_id=(y * nz + (z + k) % nz, r), device_id_type=MESH
        )
        return carry

    lax.fori_loop(1, no, greet_group, 0)
    lax.fori_loop(1, nz, greet_z, 0)

    def block(yy, zz):
        return pl.ds(pl.multiple_of((yy * nz + zz) * lm, lm), lm)

    for c in range(2):
        for q in range(ql):
            vg[c, block(y, z), q * vw : (q + 1) * vw] = v_ref[c, q]

    def operator_row(i):
        rr, rest = i // (ow * chunk), i % (ow * chunk)
        t, rest = rest // chunk, rest % chunk
        p, ii = rest // ni, rest % ni
        return (p * ow + t) * lm + rr * ni + ii

    width = min(256, modes)
    order = one_hot((rows, rows), operator_row)
    for c in range(2):
        o_copies[c].wait()

        def reorder(n, carry, c=c):
            columns = pl.ds(pl.multiple_of(n * width, width), width)
            o_buf[c, :, columns] = mm(order, o_buf[c, :, columns]).astype(BF16)
            return carry

        lax.fori_loop(0, modes // width, reorder, 0)

    pl.semaphore_wait(barrier, no - 1 + nz - 1)

    def send(src, dst, ssem, rsem, device):
        return pltpu.make_async_remote_copy(
            src_ref=src, dst_ref=dst, send_sem=ssem, recv_sem=rsem,
            device_id=device, device_id_type=MESH,
        )

    def y_first(d, yy):
        where = vg.at[0, block(yy, z), :cut]
        return send(where, where, ys0.at[d - 1], yr0.at[d - 1], (((y + d) % ny) * nz + z, r))

    def towards(way, k, incoming):
        ahead = 1 if incoming else 0
        if way == 0:
            return (z + 2 * nz - k - ahead) % nz, right
        return (z + k + ahead) % nz, left

    def ring0(way, k, d, incoming):
        zz, to = towards(way, k, incoming)
        where = vg.at[0, block((y + ny - d) % ny, zz), :cut]
        return send(where, where, zs0.at[way, k, d], zr0.at[way, k, d], (y * nz + to, r))

    def part_of(c, yy, zz):
        if c == 0:
            return vg.at[0, block(yy, zz), cut:]
        return vg.at[1, block(yy, zz)]

    def ring1(c, way, k, incoming):
        zz, to = towards(way, k, incoming)
        where = part_of(c, y, zz)
        return send(where, where, zs1.at[c, way, k], zr1.at[c, way, k], (y * nz + to, r))

    def y_last(c, d, slot, zz, incoming):
        where = part_of(c, (y + ny - d) % ny if incoming else y, zz)
        return send(
            where, where, ys1.at[c, d - 1, slot], yr1.at[c, d - 1, slot],
            (((y + d) % ny) * nz + z, r),
        )

    def relay(c, slot):
        step = jnp.where(slot % 2 == 0, 1, ny - 1)
        where = part_of(c, (y + ny - step) % ny, slot_z(slot))
        return send(
            where, where, ys1.at[c, 1, slot], yr1.at[c, 1, slot],
            (((y + step) % ny) * nz + z, r),
        )

    def relay_on(c, slot):
        for d in direct:
            y_last(c, d, slot, slot_z(slot), True).wait_recv()
        relay(c, slot).start()

    def slot_z(slot):
        return jnp.where(slot <= kr, z + nz - slot, z + slot - kr) % nz

    ways = tuple((way, steps) for way, steps in ((0, kr), (1, kl)) if steps)
    for way, steps in ways:
        ring1(0, way, 0, False).start()
    for d in range(1, ny):
        y_first(d, y).start()
    for way, steps in ways:
        ring0(way, 0, 0, False).start()
    for d in direct:
        y_last(0, d, 0, z, False).start()
    for way, steps in ways:
        ring1(1, way, 0, False).start()
    for d in range(1, ny):
        y_first(d, (y + ny - d) % ny).wait_recv()
        for way, steps in ways:
            ring0(way, 0, d, False).start()

    def ring_step(k, carry):
        for way, steps in ways:

            @pl.when(k < steps)
            def _(way=way, steps=steps):
                ring1(0, way, k, True).wait_recv()

                @pl.when(k + 1 < steps)
                def _():
                    ring1(0, way, k + 1, False).start()

                for d in direct:
                    y_last(0, d, k + 1 + (kr if way else 0), towards(way, k, True)[0], False).start()

        for way, steps in ways:

            @pl.when(k < steps)
            def _(way=way, steps=steps):
                for d in range(ny):
                    ring0(way, k, d, True).wait_recv()

                    @pl.when(k + 1 < steps)
                    def _():
                        ring0(way, k + 1, d, False).start()

                ring1(1, way, k, True).wait_recv()

                @pl.when(k + 1 < steps)
                def _():
                    ring1(1, way, k + 1, False).start()

        relay_on(0, k)

        @pl.when((k >= 1) & (k <= kl))
        def _():
            relay_on(0, k + kr)

        return carry

    lax.fori_loop(0, kr, ring_step, 0)
    relay_on(0, kr)

    def y_arrived(c, slot):
        y_last(c, 2, slot, slot_z(slot), True).wait_recv()

    def y_pass(slot):
        for d in direct:
            y_last(1, d, slot, slot_z(slot), False).start()

    def each(low, high, action):
        def body(k, carry):
            action(k)
            return carry

        lax.fori_loop(low, high, body, 0)

    each(0, nz, functools.partial(y_arrived, 0))
    each(0, nz, y_pass)

    forward = one_hot((rank, rank), lambda i: (i % vw) * ow + i // vw)
    backward = one_hot((rank, rank), lambda i: (i % ow) * vw + i // ow)

    def exchange(c, d):
        to = (r + d) % nr
        return send(
            s_buf.at[c, to], x_buf.at[c, r], as_sem.at[c, d - 1], ar_sem.at[c, d - 1], (mode, to)
        )

    def exchange_from(c, d):
        source = (r + nr - d) % nr
        return send(
            s_buf.at[c, source], x_buf.at[c, source], as_sem.at[c, d - 1], ar_sem.at[c, d - 1],
            (mode, source),
        )

    def product(c):
        mt, nt = min(256, rows), min(256, ql * vw)

        def tile(n, carry):
            a = pl.ds(pl.multiple_of((n % (rows // mt)) * mt, mt), mt)
            b = pl.ds(pl.multiple_of((n // (rows // mt)) * nt, nt), nt)
            acc[a, b] = mm(o_buf[c, a, :], vg[c, :, b])
            return carry

        lax.fori_loop(0, (rows // mt) * (ql * vw // nt), tile, 0)

        def arrange(d, carry):
            to = (r + d) % nr
            base = to * (ow * chunk)
            for t in range(ow):
                strip = acc[pl.ds(pl.multiple_of(base + t * chunk, chunk), chunk), :].astype(BF16)
                for q in range(ql):
                    s_buf[c, to, q * chunk : (q + 1) * chunk, t * vw : (t + 1) * vw] = strip[
                        :, q * vw : (q + 1) * vw
                    ]

            @pl.when(d < nr)
            def _():
                exchange(c, d).start()

            return carry

        lax.fori_loop(1, nr + 1, arrange, 0)
        x_buf[c, r] = s_buf[c, r]

    def collect(c):
        def arrived(d, carry):
            exchange_from(c, d).wait_recv()
            return carry

        lax.fori_loop(1, nr, arrived, 0)
        per = ql * chunk
        lanes = min(128, rank)
        for source in range(nr):
            for h in range(rank // lanes):
                y_buf[h, source * per : (source + 1) * per, :] = x_buf[
                    c, source, :, h * lanes : (h + 1) * lanes
                ].astype(F32)
        bh, bl = split(b_ref[c + 1])
        for i in range(ni):
            raw = jnp.concatenate(
                [y_buf[h, pl.ds(i, rank, stride=ni), :] for h in range(rank // lanes)], axis=1
            ).astype(BF16)
            now = mm(raw, forward).astype(BF16)
            p_buf[i] = now
            pt_buf[i] = mm_nt(backward, raw).astype(BF16)
            q_buf[c, :, i * u_rank : (i + 1) * u_rank] = mm_nt(now, bh) + mm_nt(now, bl)

    def partial_gram(g):
        gh, gl = split(g)
        total = None
        for i in range(ni):
            now = p_buf[i]
            wh, wl = split(mm(gh, now) + mm(gl, now))
            flipped = pt_buf[i]
            term = mm(flipped, wh) + mm(flipped, wl)
            total = term if total is None else total + term
        part[...] = total * (1.0 / (modes * rank))

    def own_rows(index):
        return pl.ds(pl.multiple_of(index * rb_rows, rb_rows), rb_rows)

    def scatter(n, k):
        other, device = group(k)
        return send(part.at[own_rows(other)], ra.at[n, o], a_s.at[n, k - 1], a_r.at[n, k - 1], device)

    def along(n, k):
        return send(
            sb.at[n], rb.at[n, z], b_s.at[n, k - 1], b_r.at[n, k - 1],
            (y * nz + (z + k) % nz, r),
        )

    def spread(n, k):
        where = gram.at[n, own_rows(o)]
        return send(where, where, c_s.at[n, k - 1], c_r.at[n, k - 1], group(k)[1])

    def solve_start(c, g):
        basis = b_ref[c]
        projected = jnp.dot(
            basis, g, precision=HIGHEST_PRECISION, preferred_element_type=F32
        )
        reduced = mm_nt(projected, basis, HIGHEST_PRECISION)
        aug[:, :head] = jnp.zeros((u_rank, head), F32)
        aug[:, :u_rank] = 0.5 * (reduced + reduced.T)
        aug[:, head:] = projected

    def solve_steps(low, high):
        row_index = lax.broadcasted_iota(jnp.int32, (u_rank, 1), 0)
        lane_index = lax.broadcasted_iota(jnp.int32, (u_rank, head), 1)

        def step(k):
            row = aug[pl.ds(k, 1), :]
            chosen = lane_index == k
            column = jnp.sum(
                jnp.where(chosen, aug[:, :head], 0.0), axis=1, keepdims=True
            )
            pivot = jnp.sum(
                jnp.where(chosen[:1], row[:, :head], 0.0), axis=1, keepdims=True
            )
            scaled = row / pivot
            aug[...] = aug[...] - jnp.where(row_index == k, 0.0, column) * scaled
            aug[pl.ds(k, 1), :] = scaled

        each(low, high, step)

    def solve_end(c):
        mh, ml = split(aug[:, head:])
        for i in range(ni):
            qh, ql_ = split(q_buf[c, :, i * u_rank : (i + 1) * u_rank])
            r_out[c, :, i, :] = mm(mh, qh) + (mm(mh, ql_) + mm(ml, qh))

    def all_reduce(n, fill_a, fill_b, fill_c):
        each(1, no, lambda k: scatter(n, k).start())
        fill_a()
        ra[n, o] = part[own_rows(o), :]
        each(
            1, no,
            lambda k: send(
                ra.at[n, group_from(k)], ra.at[n, group_from(k)],
                a_s.at[n, k - 1], a_r.at[n, k - 1], group(k)[1],
            ).wait_recv(),
        )
        total = ra[n, 0]
        for k in range(1, no):
            total = total + ra[n, k]
        sb[n] = total
        rb[n, z] = total
        each(1, nz, lambda k: along(n, k).start())
        fill_b()
        each(
            1, nz,
            lambda k: send(
                sb.at[n], rb.at[n, (z + nz - k) % nz], b_s.at[n, k - 1], b_r.at[n, k - 1],
                (y * nz + (z + k) % nz, r),
            ).wait_recv(),
        )
        total = rb[n, 0]
        for k in range(1, nz):
            total = total + rb[n, k]
        gram[n, own_rows(o), :] = total
        each(1, no, lambda k: spread(n, k).start())
        fill_c()

        def landed(k):
            where = gram.at[n, own_rows(group_from(k))]
            send(where, where, c_s.at[n, k - 1], c_r.at[n, k - 1], group(k)[1]).wait_recv()

        each(1, no, landed)
        each(1, no, lambda k: scatter(n, k).wait_send())
        each(1, nz, lambda k: along(n, k).wait_send())
        each(1, no, lambda k: spread(n, k).wait_send())

    def solve_first():
        each(0, nz, functools.partial(relay_on, 1))
        solve_start(0, g_ref[...])
        solve_steps(0, u_rank)
        solve_end(0)

    def product_second():
        each(0, nz, functools.partial(y_arrived, 1))
        product(1)

    def solve_second():
        solve_start(1, gram[0])
        solve_steps(0, u_rank // 4)

    product(0)
    collect(0)
    partial_gram(g_ref[...])
    all_reduce(0, solve_first, product_second, lambda: collect(1))
    partial_gram(gram[0])
    all_reduce(
        1, solve_second, lambda: solve_steps(u_rank // 4, u_rank), lambda: solve_end(1)
    )
    gram_out[...] = gram[1]

    for d in range(1, ny):
        y_first(d, y).wait_send()
    for way, steps in ways:

        def sent(k, way=way):
            for d in range(ny):
                ring0(way, k, d, False).wait_send()
            for c in range(2):
                ring1(c, way, k, False).wait_send()

        each(0, steps, sent)

    def y_sent(slot):
        for c in range(2):
            for d in direct:
                y_last(c, d, slot, slot_z(slot), False).wait_send()
            relay(c, slot).wait_send()

    each(0, nz, y_sent)
    for c in range(2):
        each(1, nr, lambda d, c=c: exchange(c, d).wait_send())


def shards(nr, nmode, operator_cores, vector_cores, left_gram, bases):
    cores, ow, _, lm, modes = operator_cores.shape
    ql, vw = vector_cores.shape[1:3]
    rank = left_gram.shape[0]
    ny = GRID_Y
    nz = nmode // ny
    ni = lm // nr
    rows = ow * ow * lm
    no = ny * nr
    rb_rows = rank // no
    kr = nz // 2
    dims = (ny, nz, nr, lm, ql, vw, ow, rank)
    dma = pltpu.SemaphoreType.DMA
    operator_rows = operator_cores.reshape(cores, rows, modes)
    vector_rows = vector_cores.transpose(0, 1, 3, 2)
    bases_rows = bases.transpose(0, 2, 1)
    out_rank = bases.shape[2]
    vmem = pl.BlockSpec(memory_space=pltpu.VMEM)
    pieces, gram = pl.pallas_call(
        functools.partial(window_kernel, dims),
        out_shape=(
            jax.ShapeDtypeStruct((cores, out_rank, ni, out_rank), F32),
            jax.ShapeDtypeStruct((rank, rank), F32),
        ),
        in_specs=[vmem, pl.BlockSpec(memory_space=pl.ANY), vmem, vmem],
        out_specs=(vmem, vmem),
        scratch_shapes=[
            pltpu.VMEM((cores, rows, modes), BF16),
            pltpu.VMEM((cores, modes, ql * vw), BF16),
            pltpu.VMEM((rows, ql * vw), F32),
            pltpu.VMEM((cores, nr, ql * ow * ni, rank), BF16),
            pltpu.VMEM((cores, nr, ql * ow * ni, rank), BF16),
            pltpu.VMEM((max(1, rank // 128), rank * ni, min(128, rank)), F32),
            pltpu.VMEM((ni, rank, rank), BF16),
            pltpu.VMEM((ni, rank, rank), BF16),
            pltpu.VMEM((cores, rank, ni * out_rank), F32),
            pltpu.VMEM((out_rank, 128 + rank), F32),
            pltpu.VMEM((rank, rank), F32),
            pltpu.VMEM((cores, no, rb_rows, rank), F32),
            pltpu.VMEM((cores, rb_rows, rank), F32),
            pltpu.VMEM((cores, nz, rb_rows, rank), F32),
            pltpu.VMEM((cores, rank, rank), F32),
            dma((2,)),
            dma((ny - 1,)), dma((ny - 1,)),
            dma((2, kr, ny)), dma((2, kr, ny)),
            dma((2, 2, kr)), dma((2, 2, kr)),
            dma((2, ny - 1, nz)), dma((2, ny - 1, nz)),
            dma((2, nr - 1)), dma((2, nr - 1)),
            dma((2, no - 1)), dma((2, no - 1)),
            dma((2, nz - 1)), dma((2, nz - 1)),
            dma((2, no - 1)), dma((2, no - 1)),
        ],
        compiler_params=pltpu.CompilerParams(collective_id=0, has_side_effects=True),
    )(vector_rows, operator_rows, left_gram, bases_rows)
    return pieces, gram


def solution(mesh):
    placed = (P(None, None, None, "mode", None), P(None, "rank", None, "mode"), P(), P())
    return jax.shard_map(
        functools.partial(shards, mesh.shape["rank"], mesh.shape["mode"]),
        mesh=mesh,
        in_specs=placed,
        out_specs=(P(None, None, ("mode", "rank"), None), P()),
        check_vma=False,
    )
```

```python
import functools

import jax
import jax.numpy as jnp
from jax import lax
from jax.experimental import pallas as pl
from jax.experimental.pallas import tpu as pltpu
from jax.sharding import PartitionSpec as P

GRID_Y = 4
HIGHEST_PRECISION = lax.Precision.HIGHEST
MESH = pl.DeviceIdType.MESH
F32 = jnp.float32
BF16 = jnp.bfloat16


def mm(a, b):
    return jnp.dot(a, b, preferred_element_type=F32)


def mm_nt(a, b, precision=None):
    return lax.dot_general(
        a, b, (((1,), (1,)), ((), ())), precision=precision, preferred_element_type=F32
    )


def split(a):
    high = a.astype(BF16)
    return high, (a - high.astype(F32)).astype(BF16)


def one_hot(shape, target):
    rows = lax.broadcasted_iota(jnp.int32, shape, 0)
    columns = lax.broadcasted_iota(jnp.int32, shape, 1)
    return jnp.where(target(rows) == columns, 1.0, 0.0).astype(BF16)


def window_kernel(dims, *refs):
    (ny, nz, nr, lm, ql, vw, ow, rank) = dims
    (v_ref, o_hbm, g_ref, b_ref, r_out, gram_out,
     o_buf, vg, acc, s_buf, x_buf, y_buf, p_buf, pt_buf, q_buf, aug, part, ra, sb, rb, gram,
     o_sem, ys0, yr0, zs0, zr0, zs1, zr1, ys1, yr1, as_sem, ar_sem,
     a_s, a_r, b_s, b_r, c_s, c_r) = refs
    modes = ny * nz * lm
    ni = lm // nr
    rows = ow * ow * lm
    chunk = ow * ni
    no = ny * nr
    rb_rows = rank // no
    u_rank = b_ref.shape[1]
    head = aug.shape[1] - rank
    cut = ql * vw // 4
    kr = nz // 2
    kl = nz - 1 - kr
    direct = (1, ny - 1)
    mode = lax.axis_index("mode")
    r = lax.axis_index("rank")
    y = mode // nz
    z = mode % nz
    o = y * nr + r
    right, left = (z + 1) % nz, (z + nz - 1) % nz

    def group(k):
        other = (o + k) % no
        return other, ((other // nr) * nz + z, other % nr)

    def group_from(k):
        return (o + no - k) % no

    o_copies = [
        pltpu.make_async_copy(o_hbm.at[c], o_buf.at[c], o_sem.at[c]) for c in range(2)
    ]
    for copy in o_copies:
        copy.start()

    barrier = pltpu.get_barrier_semaphore()

    def greet_group(k, carry):
        pl.semaphore_signal(barrier, inc=1, device_id=group(k)[1], device_id_type=MESH)
        return carry

    def greet_z(k, carry):
        pl.semaphore_signal(
            barrier, inc=1, device_id=(y * nz + (z + k) % nz, r), device_id_type=MESH
        )
        return carry

    lax.fori_loop(1, no, greet_group, 0)
    lax.fori_loop(1, nz, greet_z, 0)

    def block(yy, zz):
        return pl.ds(pl.multiple_of((yy * nz + zz) * lm, lm), lm)

    for c in range(2):
        for q in range(ql):
            vg[c, block(y, z), q * vw : (q + 1) * vw] = v_ref[c, q]

    def operator_row(i):
        rr, rest = i // (ow * chunk), i % (ow * chunk)
        t, rest = rest // chunk, rest % chunk
        p, ii = rest // ni, rest % ni
        return (p * ow + t) * lm + rr * ni + ii

    width = min(256, modes)
    order = one_hot((rows, rows), operator_row)

    def reorder_operator(c):
        o_copies[c].wait()

        def reorder(n, carry):
            columns = pl.ds(pl.multiple_of(n * width, width), width)
            o_buf[c, :, columns] = mm(order, o_buf[c, :, columns]).astype(BF16)
            return carry

        lax.fori_loop(0, modes // width, reorder, 0)

    pl.semaphore_wait(barrier, no - 1 + nz - 1)

    def send(src, dst, ssem, rsem, device):
        return pltpu.make_async_remote_copy(
            src_ref=src, dst_ref=dst, send_sem=ssem, recv_sem=rsem,
            device_id=device, device_id_type=MESH,
        )

    def y_first(d, yy):
        where = vg.at[0, block(yy, z), :cut]
        return send(where, where, ys0.at[d - 1], yr0.at[d - 1], (((y + d) % ny) * nz + z, r))

    def towards(way, k, incoming):
        ahead = 1 if incoming else 0
        if way == 0:
            return (z + 2 * nz - k - ahead) % nz, right
        return (z + k + ahead) % nz, left

    def ring0(way, k, d, incoming):
        zz, to = towards(way, k, incoming)
        where = vg.at[0, block((y + ny - d) % ny, zz), :cut]
        return send(where, where, zs0.at[way, k, d], zr0.at[way, k, d], (y * nz + to, r))

    def part_of(c, yy, zz):
        if c == 0:
            return vg.at[0, block(yy, zz), cut:]
        return vg.at[1, block(yy, zz)]

    def ring1(c, way, k, incoming):
        zz, to = towards(way, k, incoming)
        where = part_of(c, y, zz)
        return send(where, where, zs1.at[c, way, k], zr1.at[c, way, k], (y * nz + to, r))

    def y_last(c, d, slot, zz, incoming):
        where = part_of(c, (y + ny - d) % ny if incoming else y, zz)
        return send(
            where, where, ys1.at[c, d - 1, slot], yr1.at[c, d - 1, slot],
            (((y + d) % ny) * nz + z, r),
        )

    def relay(c, slot):
        step = jnp.where(slot % 2 == 0, 1, ny - 1)
        where = part_of(c, (y + ny - step) % ny, slot_z(slot))
        return send(
            where, where, ys1.at[c, 1, slot], yr1.at[c, 1, slot],
            (((y + step) % ny) * nz + z, r),
        )

    def relay_on(c, slot):
        for d in direct:
            y_last(c, d, slot, slot_z(slot), True).wait_recv()
        relay(c, slot).start()

    def slot_z(slot):
        return jnp.where(slot <= kr, z + nz - slot, z + slot - kr) % nz

    ways = tuple((way, steps) for way, steps in ((0, kr), (1, kl)) if steps)
    for way, steps in ways:
        ring1(0, way, 0, False).start()
    for d in range(1, ny):
        y_first(d, y).start()
    for way, steps in ways:
        ring0(way, 0, 0, False).start()
    for d in direct:
        y_last(0, d, 0, z, False).start()
    for way, steps in ways:
        ring1(1, way, 0, False).start()
    for d in range(1, ny):
        y_first(d, (y + ny - d) % ny).wait_recv()
        for way, steps in ways:
            ring0(way, 0, d, False).start()

    def ring_step(k, carry):
        for way, steps in ways:

            @pl.when(k < steps)
            def _(way=way, steps=steps):
                ring1(0, way, k, True).wait_recv()

                @pl.when(k + 1 < steps)
                def _():
                    ring1(0, way, k + 1, False).start()

                for d in direct:
                    y_last(0, d, k + 1 + (kr if way else 0), towards(way, k, True)[0], False).start()

        for way, steps in ways:

            @pl.when(k < steps)
            def _(way=way, steps=steps):
                for d in range(ny):
                    ring0(way, k, d, True).wait_recv()

                    @pl.when(k + 1 < steps)
                    def _():
                        ring0(way, k + 1, d, False).start()

                ring1(1, way, k, True).wait_recv()

                @pl.when(k + 1 < steps)
                def _():
                    ring1(1, way, k + 1, False).start()

        relay_on(0, k)

        @pl.when((k >= 1) & (k <= kl))
        def _():
            relay_on(0, k + kr)

        return carry

    lax.fori_loop(0, kr, ring_step, 0)
    relay_on(0, kr)

    def y_arrived(c, slot):
        y_last(c, 2, slot, slot_z(slot), True).wait_recv()

    def y_pass(slot):
        for d in direct:
            y_last(1, d, slot, slot_z(slot), False).start()

    def each(low, high, action):
        def body(k, carry):
            action(k)
            return carry

        lax.fori_loop(low, high, body, 0)

    each(0, nz, functools.partial(y_arrived, 0))
    each(0, nz, y_pass)

    forward = one_hot((rank, rank), lambda i: (i % vw) * ow + i // vw)
    backward = one_hot((rank, rank), lambda i: (i % ow) * vw + i // ow)

    def exchange(c, d):
        to = (r + d) % nr
        return send(
            s_buf.at[c, to], x_buf.at[c, r], as_sem.at[c, d - 1], ar_sem.at[c, d - 1], (mode, to)
        )

    def exchange_from(c, d):
        source = (r + nr - d) % nr
        return send(
            s_buf.at[c, source], x_buf.at[c, source], as_sem.at[c, d - 1], ar_sem.at[c, d - 1],
            (mode, source),
        )

    def product(c):
        mt, nt = min(256, rows), min(256, ql * vw)

        def tile(n, carry):
            a = pl.ds(pl.multiple_of((n % (rows // mt)) * mt, mt), mt)
            b = pl.ds(pl.multiple_of((n // (rows // mt)) * nt, nt), nt)
            acc[a, b] = mm(o_buf[c, a, :], vg[c, :, b])
            return carry

        lax.fori_loop(0, (rows // mt) * (ql * vw // nt), tile, 0)

        def arrange(d, carry):
            to = (r + d) % nr
            base = to * (ow * chunk)
            for t in range(ow):
                strip = acc[pl.ds(pl.multiple_of(base + t * chunk, chunk), chunk), :].astype(BF16)
                for q in range(ql):
                    s_buf[c, to, q * chunk : (q + 1) * chunk, t * vw : (t + 1) * vw] = strip[
                        :, q * vw : (q + 1) * vw
                    ]

            @pl.when(d < nr)
            def _():
                exchange(c, d).start()

            return carry

        lax.fori_loop(1, nr + 1, arrange, 0)
        x_buf[c, r] = s_buf[c, r]

    def collect(c):
        def arrived(d, carry):
            exchange_from(c, d).wait_recv()
            return carry

        lax.fori_loop(1, nr, arrived, 0)
        per = ql * chunk
        lanes = min(128, rank)
        for source in range(nr):
            for h in range(rank // lanes):
                y_buf[h, source * per : (source + 1) * per, :] = x_buf[
                    c, source, :, h * lanes : (h + 1) * lanes
                ].astype(F32)
        bh, bl = split(b_ref[c + 1])
        for i in range(ni):
            raw = jnp.concatenate(
                [y_buf[h, pl.ds(i, rank, stride=ni), :] for h in range(rank // lanes)], axis=1
            ).astype(BF16)
            now = mm(raw, forward).astype(BF16)
            p_buf[i] = now
            pt_buf[i] = mm_nt(backward, raw).astype(BF16)
            q_buf[c, :, i * u_rank : (i + 1) * u_rank] = mm_nt(now, bh) + mm_nt(now, bl)

    def partial_gram(g):
        gh, gl = split(g)
        total = None
        for i in range(ni):
            now = p_buf[i]
            wh, wl = split(mm(gh, now) + mm(gl, now))
            flipped = pt_buf[i]
            term = mm(flipped, wh) + mm(flipped, wl)
            total = term if total is None else total + term
        part[...] = total * (1.0 / (modes * rank))

    def own_rows(index):
        return pl.ds(pl.multiple_of(index * rb_rows, rb_rows), rb_rows)

    def scatter(n, k):
        other, device = group(k)
        return send(part.at[own_rows(other)], ra.at[n, o], a_s.at[n, k - 1], a_r.at[n, k - 1], device)

    def along(n, k):
        return send(
            sb.at[n], rb.at[n, z], b_s.at[n, k - 1], b_r.at[n, k - 1],
            (y * nz + (z + k) % nz, r),
        )

    def spread(n, k):
        where = gram.at[n, own_rows(o)]
        return send(where, where, c_s.at[n, k - 1], c_r.at[n, k - 1], group(k)[1])

    def solve_start(c, g):
        basis = b_ref[c]
        projected = jnp.dot(
            basis, g, precision=HIGHEST_PRECISION, preferred_element_type=F32
        )
        reduced = mm_nt(projected, basis, HIGHEST_PRECISION)
        aug[:, :head] = jnp.zeros((u_rank, head), F32)
        aug[:, :u_rank] = 0.5 * (reduced + reduced.T)
        aug[:, head:] = projected

    def solve_steps(low, high):
        row_index = lax.broadcasted_iota(jnp.int32, (u_rank, 1), 0)
        lane_index = lax.broadcasted_iota(jnp.int32, (u_rank, head), 1)

        def step(k):
            row = aug[pl.ds(k, 1), :]
            chosen = lane_index == k
            column = jnp.sum(
                jnp.where(chosen, aug[:, :head], 0.0), axis=1, keepdims=True
            )
            pivot = jnp.sum(
                jnp.where(chosen[:1], row[:, :head], 0.0), axis=1, keepdims=True
            )
            scaled = row / pivot
            aug[...] = aug[...] - jnp.where(row_index == k, 0.0, column) * scaled
            aug[pl.ds(k, 1), :] = scaled

        each(low, high, step)

    def solve_end(c):
        mh, ml = split(aug[:, head:])
        for i in range(ni):
            qh, ql_ = split(q_buf[c, :, i * u_rank : (i + 1) * u_rank])
            r_out[c, :, i, :] = mm(mh, qh) + (mm(mh, ql_) + mm(ml, qh))

    def all_reduce(n, fill_a, fill_b, fill_c):
        each(1, no, lambda k: scatter(n, k).start())
        fill_a()
        ra[n, o] = part[own_rows(o), :]
        each(
            1, no,
            lambda k: send(
                ra.at[n, group_from(k)], ra.at[n, group_from(k)],
                a_s.at[n, k - 1], a_r.at[n, k - 1], group(k)[1],
            ).wait_recv(),
        )
        total = ra[n, 0]
        for k in range(1, no):
            total = total + ra[n, k]
        sb[n] = total
        rb[n, z] = total
        each(1, nz, lambda k: along(n, k).start())
        fill_b()
        each(
            1, nz,
            lambda k: send(
                sb.at[n], rb.at[n, (z + nz - k) % nz], b_s.at[n, k - 1], b_r.at[n, k - 1],
                (y * nz + (z + k) % nz, r),
            ).wait_recv(),
        )
        total = rb[n, 0]
        for k in range(1, nz):
            total = total + rb[n, k]
        gram[n, own_rows(o), :] = total
        each(1, no, lambda k: spread(n, k).start())
        fill_c()

        def landed(k):
            where = gram.at[n, own_rows(group_from(k))]
            send(where, where, c_s.at[n, k - 1], c_r.at[n, k - 1], group(k)[1]).wait_recv()

        each(1, no, landed)
        each(1, no, lambda k: scatter(n, k).wait_send())
        each(1, nz, lambda k: along(n, k).wait_send())
        each(1, no, lambda k: spread(n, k).wait_send())

    def solve_first():
        each(0, nz, functools.partial(relay_on, 1))
        solve_start(0, g_ref[...])
        solve_steps(0, u_rank)
        solve_end(0)

    def product_second():
        reorder_operator(1)
        each(0, nz, functools.partial(y_arrived, 1))
        product(1)

    def solve_second():
        solve_start(1, gram[0])
        solve_steps(0, u_rank // 4)

    reorder_operator(0)
    product(0)
    collect(0)
    partial_gram(g_ref[...])
    all_reduce(0, solve_first, product_second, lambda: collect(1))
    partial_gram(gram[0])
    all_reduce(
        1, solve_second, lambda: solve_steps(u_rank // 4, u_rank), lambda: solve_end(1)
    )
    gram_out[...] = gram[1]

    for d in range(1, ny):
        y_first(d, y).wait_send()
    for way, steps in ways:

        def sent(k, way=way):
            for d in range(ny):
                ring0(way, k, d, False).wait_send()
            for c in range(2):
                ring1(c, way, k, False).wait_send()

        each(0, steps, sent)

    def y_sent(slot):
        for c in range(2):
            for d in direct:
                y_last(c, d, slot, slot_z(slot), False).wait_send()
            relay(c, slot).wait_send()

    each(0, nz, y_sent)
    for c in range(2):
        each(1, nr, lambda d, c=c: exchange(c, d).wait_send())


def shards(nr, nmode, operator_cores, vector_cores, left_gram, bases):
    cores, ow, _, lm, modes = operator_cores.shape
    ql, vw = vector_cores.shape[1:3]
    rank = left_gram.shape[0]
    ny = GRID_Y
    nz = nmode // ny
    ni = lm // nr
    rows = ow * ow * lm
    no = ny * nr
    rb_rows = rank // no
    kr = nz // 2
    dims = (ny, nz, nr, lm, ql, vw, ow, rank)
    dma = pltpu.SemaphoreType.DMA
    operator_rows = operator_cores.reshape(cores, rows, modes)
    vector_rows = vector_cores.transpose(0, 1, 3, 2)
    bases_rows = bases.transpose(0, 2, 1)
    out_rank = bases.shape[2]
    vmem = pl.BlockSpec(memory_space=pltpu.VMEM)
    pieces, gram = pl.pallas_call(
        functools.partial(window_kernel, dims),
        out_shape=(
            jax.ShapeDtypeStruct((cores, out_rank, ni, out_rank), F32),
            jax.ShapeDtypeStruct((rank, rank), F32),
        ),
        in_specs=[vmem, pl.BlockSpec(memory_space=pl.ANY), vmem, vmem],
        out_specs=(vmem, vmem),
        scratch_shapes=[
            pltpu.VMEM((cores, rows, modes), BF16),
            pltpu.VMEM((cores, modes, ql * vw), BF16),
            pltpu.VMEM((rows, ql * vw), F32),
            pltpu.VMEM((cores, nr, ql * ow * ni, rank), BF16),
            pltpu.VMEM((cores, nr, ql * ow * ni, rank), BF16),
            pltpu.VMEM((max(1, rank // 128), rank * ni, min(128, rank)), F32),
            pltpu.VMEM((ni, rank, rank), BF16),
            pltpu.VMEM((ni, rank, rank), BF16),
            pltpu.VMEM((cores, rank, ni * out_rank), F32),
            pltpu.VMEM((out_rank, 128 + rank), F32),
            pltpu.VMEM((rank, rank), F32),
            pltpu.VMEM((cores, no, rb_rows, rank), F32),
            pltpu.VMEM((cores, rb_rows, rank), F32),
            pltpu.VMEM((cores, nz, rb_rows, rank), F32),
            pltpu.VMEM((cores, rank, rank), F32),
            dma((2,)),
            dma((ny - 1,)), dma((ny - 1,)),
            dma((2, kr, ny)), dma((2, kr, ny)),
            dma((2, 2, kr)), dma((2, 2, kr)),
            dma((2, ny - 1, nz)), dma((2, ny - 1, nz)),
            dma((2, nr - 1)), dma((2, nr - 1)),
            dma((2, no - 1)), dma((2, no - 1)),
            dma((2, nz - 1)), dma((2, nz - 1)),
            dma((2, no - 1)), dma((2, no - 1)),
        ],
        compiler_params=pltpu.CompilerParams(collective_id=0, has_side_effects=True),
    )(vector_rows, operator_rows, left_gram, bases_rows)
    return pieces, gram


def solution(mesh):
    placed = (P(None, None, None, "mode", None), P(None, "rank", None, "mode"), P(), P())
    return jax.shard_map(
        functools.partial(shards, mesh.shape["rank"], mesh.shape["mode"]),
        mesh=mesh,
        in_specs=placed,
        out_specs=(P(None, None, ("mode", "rank"), None), P()),
        check_vma=False,
    )
```
